32 devices in a mesh: src: 8 (over z, x), dst: 4 (over y, core).
Axes of the slice: x: 2, y: 2, z: 4, core: 2. Of those that a mesh axis runs over, the one named last changes fastest.
Arguments:
- values: bfloat16 [256, 32, 128, 128], P(('src', 'dst')), may hold values from -6 to 6
- until: int32 [256, 128, 128], P(('src', 'dst')), may hold values from 0 to 32
- blocks: int32 [256, 3], P(('src', 'dst')), may hold values from 0 to 255, as said below
- count: int32 [32], P(('src', 'dst')), may hold values from 1 to 8, as said below
- a_factor: bfloat16 [64, 32768], P('dst', 'src'), may hold values from -6 to 6
- b_factor: bfloat16 [64, 16384], P('src', 'dst'), may hold values from -6 to 6
- c_factor: bfloat16 [32, 256], P(None, ('src', 'dst')), may hold values from -6 to 6
- core: float32 [64, 64, 32], replicated, may hold values from -0.0048828125 to 0.0048828125
Outputs:
- ttmc_t: float32 [64, 32768], P('dst', 'src')
The draws below stay inside these ranges and needn't reach their ends.
Inputs may be any that keep to these rules, and one draw needn't show every extreme that they name: Rows of blocks come 8 to a device, devices in the order of src then dst; the rows of device (p, q) name source blocks p * 32 to p * 32 + 31, destination blocks q * 32 to q * 32 + 31 and hour blocks below 8, no block twice on a device, and every row names such a block even where its slot is not live. `count`: entry p * 4 + q counts the live slots of device (p, q), which are its first ones; some device has all 8 live.
All inputs are finite; a program needn't handle non-finite values.
Results may differ from the reference program's by a relative error of at most 0.0003.
Values may be sent and summed in bfloat16 or wider, within the bound.
A program may use at most 128 MiB of HBM per device.

```python
import jax
import jax.numpy as jnp
from jax import lax

R1 = 64
R2 = 64
R3 = 32
BI = 128
BJ = 128
BT = 32
SB_DEV = 32
DB_DEV = 32
NTB = 8
CAP = 8
NSB = 256
NDB = 128
ROWS = 32768
COLS = 16384
HOURS = 256
SLOTS = 256
N_SRC = 8
N_DST = 4


def draw_blocks(key, part):
    devices = N_SRC * N_DST
    positions = SB_DEV * DB_DEV * NTB
    scores = jax.random.randint(jax.random.fold_in(key, 11), (devices, positions), 0, 4096)
    scores = scores * positions + jnp.arange(positions, dtype=jnp.int32)[None, :]
    device_grid = jnp.arange(devices, dtype=jnp.int32)[:, None]
    position_grid = jnp.arange(positions, dtype=jnp.int32)[None, :]
    forced = (device_grid == devices - 1) & (position_grid == positions - 1)
    scores = jnp.where(forced, jnp.full_like(scores, -1), scores)
    chosen = jnp.argsort(scores, axis=1, stable=True)[:, :CAP].astype(jnp.int32)
    device_ids = jnp.arange(devices, dtype=jnp.int32)[:, None]
    src_pos = device_ids // N_DST
    dst_pos = device_ids % N_DST
    source_block = src_pos * SB_DEV + chosen // (DB_DEV * NTB)
    target_block = dst_pos * DB_DEV + chosen // NTB % DB_DEV
    hour_block = chosen % NTB
    stacked = jnp.stack([source_block, target_block, hour_block], axis=-1)
    return stacked.reshape(devices * CAP, 3).astype(jnp.int32)


def draw_count(key, part):
    devices = N_SRC * N_DST
    raw_draw = jax.random.randint(jax.random.fold_in(key, 23), (devices,), 0, CAP)
    counted = 1 + raw_draw * raw_draw // CAP
    busiest = jax.random.randint(jax.random.fold_in(key, 29), (), 0, devices)
    full_cap = jnp.full((devices,), CAP, jnp.int32)
    return jnp.where(jnp.arange(devices, dtype=jnp.int32) == busiest, full_cap, counted).astype(jnp.int32)


def plant(array, stream_key, smallest, top_value):
    longest = array.shape.index(max(array.shape))
    spots = []
    for shift in (0, 1):
        where = [jax.random.randint(jax.random.fold_in(stream_key, axis), (), 0, length) for axis, length in enumerate(array.shape)]
        where[longest] = (where[longest] + shift) % array.shape[longest]
        spots.append(tuple(where))
    return array.at[spots[0]].set(smallest).at[spots[1]].set(top_value)


def levels(key, dims, pieces, smallest, largest):
    level = 1.0
    for dim, blocks in pieces:
        steps = jax.random.uniform(jax.random.fold_in(jax.random.fold_in(key, 6), dim), (blocks,), jnp.float32, smallest / len(pieces), largest / len(pieces))
        level = level * jnp.repeat(jnp.exp(steps), dims[dim] // blocks).reshape((-1,) + (1,) * (len(dims) - 1 - dim))
    return level


def bell_draw(rng, extent, spread, limit, cuts=(), kind=jnp.bfloat16):
    values = spread * jax.random.normal(rng, extent, jnp.float32)
    if cuts:
        values = values * levels(rng, extent, cuts, -0.22, 0.18)
    return jnp.clip(values, -limit, limit).astype(kind)


def setup_inputs(seed: int = 0) -> dict:
    seeds = jax.random.split(jax.random.key(seed), 9)
    values = bell_draw(seeds[0], (SLOTS, BT, BI, BJ), 1.0, 6.0, ((0, 32),))
    until = plant(jax.random.randint(seeds[1], (SLOTS, BI, BJ), 0, BT + 1), jax.random.fold_in(seeds[1], 1), 0, BT).astype(jnp.int32)
    blocks = draw_blocks(jax.random.fold_in(seeds[8], 71), 0)
    count = draw_count(jax.random.fold_in(seeds[8], 71), 0)
    a_factor = bell_draw(seeds[4], (R1, ROWS), 1.0, 6.0, ((0, 4), (1, 8)))
    b_factor = bell_draw(seeds[5], (R2, COLS), 1.0, 6.0, ((0, 8), (1, 4)))
    c_factor = bell_draw(seeds[6], (R3, HOURS), 1.0, 6.0, ((1, 32),))
    core = bell_draw(seeds[7], (R1, R2, R3), ((R2 * R3 * BJ * BT) ** -0.5), 0.0048828125, (), jnp.float32)
    return dict(values=values, until=until, blocks=blocks, count=count, a_factor=a_factor, b_factor=b_factor, c_factor=c_factor, core=core)


highest = lax.Precision.HIGHEST


def reference(values, until, blocks, count, a_factor, b_factor, c_factor, core):
    rank_a, rank_b, rank_c = core.shape
    a_wide = a_factor.astype(jnp.float32).reshape(rank_a, NSB, BI)
    b_narrow = b_factor.reshape(rank_b, NDB, BJ)
    c_wide = c_factor.astype(jnp.float32).reshape(rank_c, NTB, BT)
    slot_ids = jnp.arange(values.shape[0], dtype=jnp.int32)
    live_slots = (slot_ids % CAP) < count[slot_ids // CAP]
    hour_ids = jnp.arange(BT, dtype=jnp.int32)

    def per_block(running, item):
        block_vals, hour_limit, where_at, is_live = item
        a_rows = lax.dynamic_index_in_dim(a_wide, where_at[0], 1, keepdims=False)
        b_rows = lax.dynamic_index_in_dim(b_narrow, where_at[1], 1, keepdims=False).astype(jnp.float32)
        c_rows = lax.dynamic_index_in_dim(c_wide, where_at[2], 1, keepdims=False)
        first = jnp.einsum("abk,kt->tab", core, c_rows, precision=highest)
        second = jnp.einsum("tab,bj->atj", first, b_rows, precision=highest)
        rebuilt = jnp.einsum("ai,atj->tij", a_rows, second, precision=highest)
        observed = hour_ids[:, None, None] < hour_limit[None, :, :]
        imputed = jnp.where(observed, block_vals.astype(jnp.float32), rebuilt).astype(jnp.bfloat16)
        imputed = lax.optimization_barrier(imputed)
        along_dst = jnp.einsum("tij,bj->bti", imputed.astype(jnp.float32), b_rows, precision=highest)
        inner_sum = jnp.einsum("bti,kt->bki", along_dst, c_rows, precision=highest)
        slot_share = jnp.einsum("bki,abk->ai", inner_sum, core, precision=highest)
        slot_share = jnp.where(is_live, slot_share, jnp.zeros_like(slot_share))
        row_start = where_at[0].astype(jnp.int32)
        anchor = jnp.zeros((), jnp.int32)
        current = lax.dynamic_slice(running, (anchor, row_start, anchor), (rank_a, 1, BI))
        running = lax.dynamic_update_slice(running, current + slot_share[:, None, :], (anchor, row_start, anchor))
        return running, None

    running = jnp.zeros((rank_a, NSB, BI), jnp.float32)
    running, _ = lax.scan(per_block, running, (values, until, blocks, live_slots))
    return running.reshape(rank_a, NSB * BI)
```

```python
import functools

import jax
import jax.numpy as jnp
from jax import lax
from jax.experimental import pallas as pl
from jax.experimental.pallas import tpu as pltpu
from jax.sharding import PartitionSpec as P

BI = 128
BJ = 128
BT = 32
MESH = pl.DeviceIdType.MESH


def greet(n_src, n_dst):
    src, dst = lax.axis_index("src"), lax.axis_index("dst")
    barrier = pltpu.get_barrier_semaphore()
    for step in range(1, n_dst):
        peer = (src, lax.rem(dst + step, n_dst))
        pl.semaphore_signal(barrier, inc=1, device_id=peer, device_id_type=MESH)
    for step in range(1, n_src):
        peer = (lax.rem(src + step, n_src), dst)
        pl.semaphore_signal(barrier, inc=1, device_id=peer, device_id_type=MESH)
    pl.semaphore_wait(barrier, n_dst - 1 + n_src - 1)
    return src, dst


def gather_kernel(n_src, n_dst, a_ref, b_ref, c_ref, a_all, b_all, c_all,
                  own_sem, a_send, a_recv, b_send, b_recv, c_send, c_recv, h_send, h_recv):
    src, dst = lax.axis_index("src"), lax.axis_index("dst")
    own = [
        pltpu.make_async_copy(a_ref, a_all.at[dst], own_sem.at[0]),
        pltpu.make_async_copy(b_ref, b_all.at[src], own_sem.at[1]),
        pltpu.make_async_copy(c_ref, c_all.at[src, dst], own_sem.at[2]),
    ]
    for copy in own:
        copy.start()
    greet(n_src, n_dst)

    def remote(source, target, send, recv, peer):
        return pltpu.make_async_remote_copy(
            src_ref=source, dst_ref=target, send_sem=send, recv_sem=recv,
            device_id=peer, device_id_type=MESH)

    hours, wide, tall = [], [], []
    for step in range(1, n_src):
        peer = (lax.rem(src + step, n_src), dst)
        hours.append(remote(c_ref, c_all.at[src, dst], c_send.at[step - 1], c_recv.at[step - 1], peer))
        hours[-1].start()
    for step in range(1, n_src):
        peer = (lax.rem(src + step, n_src), dst)
        wide.append(remote(b_ref, b_all.at[src], b_send.at[step - 1], b_recv.at[step - 1], peer))
        wide[-1].start()
    for step in range(1, n_dst):
        peer = (src, lax.rem(dst + step, n_dst))
        tall.append(remote(a_ref, a_all.at[dst], a_send.at[step - 1], a_recv.at[step - 1], peer))
        tall[-1].start()
    for copy in own:
        copy.wait()
    for copy in hours:
        copy.wait()
    rest = []
    for step in range(1, n_dst):
        peer = (src, lax.rem(dst + step, n_dst))
        rest.append(remote(c_all.at[:, dst], c_all.at[:, dst], h_send.at[step - 1], h_recv.at[step - 1], peer))
        rest[-1].start()
    for copy in wide + tall + rest:
        copy.wait()


def gather_all(n_src, n_dst, a, b, c):
    vmem = pl.BlockSpec(memory_space=pltpu.VMEM)
    dma = pltpu.SemaphoreType.DMA
    return pl.pallas_call(
        functools.partial(gather_kernel, n_src, n_dst),
        out_shape=(
            jax.ShapeDtypeStruct((n_dst,) + a.shape, a.dtype),
            jax.ShapeDtypeStruct((n_src,) + b.shape, b.dtype),
            jax.ShapeDtypeStruct((n_src, n_dst) + c.shape, c.dtype),
        ),
        in_specs=[vmem] * 3,
        out_specs=(vmem,) * 3,
        scratch_shapes=[
            dma((3,)), dma((n_dst - 1,)), dma((n_dst - 1,)), dma((n_src - 1,)), dma((n_src - 1,)),
            dma((n_src - 1,)), dma((n_src - 1,)), dma((n_dst - 1,)), dma((n_dst - 1,)),
        ],
        compiler_params=pltpu.CompilerParams(collective_id=0, has_side_effects=True),
        name="gather_factors",
    )(a, b, c)


def split(x):
    high = x.astype(jnp.bfloat16)
    return high, (x - high.astype(jnp.float32)).astype(jnp.bfloat16)


def dot(x, y, contract):
    return lax.dot_general(x, y, (contract, ((), ())), preferred_element_type=jnp.float32)


NN = ((1,), (0,))
NT = ((1,), (1,))
CHUNK = 8


def slot_kernel(n_dst, where_ref, count_ref, values_ref, until_ref, a_ref, b_ref, c_ref, core_ref,
                out_ref, first_ref, a_rows):
    n = pl.program_id(0)
    rank_a = a_rows.shape[0]
    half = rank_a // 2
    each = rank_a // n_dst

    @pl.when(n >= count_ref[0])
    def _():
        out_ref[...] = jnp.zeros_like(out_ref)

    @pl.when(n < count_ref[0])
    def _():
        hour = where_ref[n, 2]
        c_rows = c_ref[pl.ds(pl.multiple_of(hour * BT, BT), BT), :]
        first = dot(c_rows, core_ref[...], NT)
        for pair in range(half):
            first_ref[pl.ds(pair, BT, stride=half), :] = first[:, pair * 128:(pair + 1) * 128]
        b = b_ref[...]
        none = jnp.zeros_like(b)
        b_top = jnp.concatenate([b, none], axis=1)
        b_low = jnp.concatenate([none, b], axis=1)
        b_wide = jnp.concatenate([b_top, b_low, b_top, b_low], axis=0)
        a_rows[...] = a_ref[...].astype(jnp.float32)
        a_even = a_rows[pl.ds(0, half, stride=2), :]
        a_odd = a_rows[pl.ds(1, half, stride=2), :]
        a_cols = jnp.concatenate([a_even, a_odd, a_even, a_odd], axis=0).T.astype(jnp.bfloat16)
        lane = lax.broadcasted_iota(jnp.int32, (half, 128), 1)
        left = lane < 64
        until = until_ref[0]

        def step(chunk, total):
            start = chunk * CHUNK
            f = first_ref[pl.ds(pl.multiple_of(start * half, half), CHUNK * half), :]
            f_high, f_low = split(f)
            second = dot(jnp.concatenate([f_high, f_low], axis=1), b_wide, NN)
            s_high, s_low = split(second)
            for two in range(0, CHUNK, 2):
                def column(t):
                    rows = slice(t * half, (t + 1) * half)
                    return jnp.concatenate(
                        [s_high[rows, :128], s_high[rows, 128:], s_low[rows, :128], s_low[rows, 128:]], axis=0)
                rebuilt = dot(a_cols, jnp.concatenate([column(two), column(two + 1)], axis=1), NN)
                parts = []
                for side in range(2):
                    seen = values_ref[0, start + two + side].astype(jnp.float32)
                    guess = rebuilt[:, side * 128:(side + 1) * 128]
                    parts.append(jnp.where(start + two + side < until, seen, guess).astype(jnp.bfloat16))
                along = dot(b, jnp.concatenate(parts, axis=0), NT)
                along_high, along_low = split(along)
                core_high, core_low, turn_high, turn_low = [], [], [], []
                for side in range(2):
                    rows = slice((two + side) * half, (two + side + 1) * half)
                    cols = slice(side * 128, (side + 1) * 128)
                    fh, fl = f_high[rows], f_low[rows]
                    nil = jnp.zeros_like(fh)
                    core_high.append(jnp.concatenate([jnp.where(left, fh, nil), jnp.where(left, nil, fh)], axis=0))
                    core_low.append(jnp.concatenate([jnp.where(left, fl, nil), jnp.where(left, nil, fl)], axis=0))
                    turn_high += [along_high[:, cols]] * 2
                    turn_low += [along_low[:, cols]] * 2
                turn_high = jnp.concatenate(turn_high, axis=0)
                turn_low = jnp.concatenate(turn_low, axis=0)
                core_high = jnp.concatenate(core_high, axis=1)
                core_low = jnp.concatenate(core_low, axis=1)
                both = dot(jnp.concatenate([core_high, core_low], axis=0), turn_high, NN)
                total = total + both[:rank_a] + both[rank_a:] + dot(core_high, turn_low, NN)
            return total

        total = lax.fori_loop(0, BT // CHUNK, step, jnp.zeros((rank_a, BI), jnp.float32))
        a_rows[pl.ds(0, half, stride=2), :] = total[:half]
        a_rows[pl.ds(1, half, stride=2), :] = total[half:]
        for q in range(n_dst):
            out_ref[q, 0] = a_rows[q * each:(q + 1) * each, :]


def slot_shares(n_dst, where, count, values, until, a, b, c, core):
    slots = values.shape[0]
    rank_a = a.shape[0]

    def alive(n, count_ref):
        return jnp.minimum(n, count_ref[0] - 1)

    return pl.pallas_call(
        functools.partial(slot_kernel, n_dst),
        out_shape=jax.ShapeDtypeStruct((n_dst, slots, rank_a // n_dst, BI), jnp.float32),
        grid_spec=pltpu.PrefetchScalarGridSpec(
            num_scalar_prefetch=2,
            grid=(slots,),
            in_specs=[
                pl.BlockSpec((1, BT, BI, BJ), lambda n, w, c: (alive(n, c), 0, 0, 0)),
                pl.BlockSpec((1, BI, BJ), lambda n, w, c: (alive(n, c), 0, 0)),
                pl.BlockSpec((rank_a, BI), lambda n, w, c: (0, w[alive(n, c), 0])),
                pl.BlockSpec((b.shape[0], BJ), lambda n, w, c: (0, w[alive(n, c), 1])),
                pl.BlockSpec(c.shape, lambda n, w, c: (0, 0)),
                pl.BlockSpec(core.shape, lambda n, w, c: (0, 0)),
            ],
            out_specs=pl.BlockSpec((n_dst, 1, rank_a // n_dst, BI), lambda n, w, c: (0, n, 0, 0)),
            scratch_shapes=[
                pltpu.VMEM((BT * rank_a // 2, 128), jnp.float32),
                pltpu.VMEM((rank_a, BI), jnp.float32),
            ],
        ),
        name="slot_shares",
    )(where, count, values, until, a, b, c, core)


def sum_kernel(n_dst, share_ref, ids_ref, out_ref, shares, ids, own_sem, s_send, s_recv, i_send, i_recv):
    src, dst = lax.axis_index("src"), lax.axis_index("dst")
    own = [
        pltpu.make_async_copy(share_ref.at[dst], shares.at[dst], own_sem.at[0]),
        pltpu.make_async_copy(ids_ref, ids.at[dst], own_sem.at[1]),
    ]
    for copy in own:
        copy.start()
    greet(1, n_dst)
    copies = []
    for step in range(1, n_dst):
        to = lax.rem(dst + step, n_dst)
        for source, target, send, recv in (
            (share_ref.at[to], shares.at[dst], s_send, s_recv),
            (ids_ref, ids.at[dst], i_send, i_recv),
        ):
            copies.append(pltpu.make_async_remote_copy(
                src_ref=source, dst_ref=target, send_sem=send.at[step - 1], recv_sem=recv.at[step - 1],
                device_id=(src, to), device_id_type=MESH))
            copies[-1].start()
    for copy in own + copies:
        copy.wait()
    slots, each = shares.shape[1], shares.shape[2]

    def block(s, carry):
        def device(q, total):
            for n in range(slots):
                mine = jnp.broadcast_to(ids[q, n:n + 1, :], (each, BI)) == s
                total = total + jnp.where(mine, shares[q, n], 0.0)
            return total
        total = jnp.zeros((each, BI), jnp.float32)
        total = lax.fori_loop(0, n_dst, device, total)
        out_ref[:, pl.ds(pl.multiple_of(s * BI, BI), BI)] = total
        return carry

    lax.fori_loop(0, out_ref.shape[1] // BI, block, 0)


def sum_shares(n_dst, shares, ids, columns):
    vmem = pl.BlockSpec(memory_space=pltpu.VMEM)
    dma = pltpu.SemaphoreType.DMA
    return pl.pallas_call(
        functools.partial(sum_kernel, n_dst),
        out_shape=jax.ShapeDtypeStruct((shares.shape[2], columns), jnp.float32),
        in_specs=[vmem] * 2,
        out_specs=vmem,
        scratch_shapes=[
            pltpu.VMEM(shares.shape, jnp.float32),
            pltpu.VMEM((n_dst,) + ids.shape, jnp.int32),
            dma((2,)), dma((n_dst - 1,)), dma((n_dst - 1,)), dma((n_dst - 1,)), dma((n_dst - 1,)),
        ],
        compiler_params=pltpu.CompilerParams(collective_id=1, has_side_effects=True),
        name="sum_shares",
    )(shares, ids)


def on_device(n_src, n_dst, values, until, blocks, count, a_factor, b_factor, c_factor, core):
    rank_a, rank_b, rank_c = core.shape
    slots = values.shape[0]
    src_blocks = a_factor.shape[1] // BI
    dst_blocks = b_factor.shape[1] // BJ
    base = jnp.stack([
        lax.axis_index("src") * src_blocks, lax.axis_index("dst") * dst_blocks, jnp.zeros((), jnp.int32)])
    where = blocks - base.astype(jnp.int32)[None, :]
    flat = core.reshape(rank_a * rank_b, rank_c)
    high = lax.reduce_precision(flat, 8, 7)
    rest = flat - high
    mid = lax.reduce_precision(rest, 8, 7)
    core_parts = jnp.concatenate([high, mid, rest - mid], axis=1).astype(jnp.bfloat16)
    a_all, b_all, c_all = gather_all(n_src, n_dst, a_factor, b_factor, c_factor.T.astype(jnp.float32))
    a_all = a_all.reshape(rank_a, -1)
    b_all = b_all.reshape(rank_b, -1)
    c_all = c_all.reshape(-1, rank_c).astype(jnp.bfloat16)
    c_all = jnp.concatenate([c_all] * 3, axis=1)
    shares = slot_shares(n_dst, where, count, values, until, a_all, b_all, c_all, core_parts)
    live = jnp.arange(slots, dtype=jnp.int32) < count[0]
    ids = jnp.broadcast_to(jnp.where(live, where[:, 0], -1)[:, None], (slots, BI))
    return sum_shares(n_dst, shares, ids, a_factor.shape[1])


def solution(mesh):
    return jax.shard_map(
        functools.partial(on_device, mesh.shape["src"], mesh.shape["dst"]),
        mesh=mesh,
        in_specs=(
            P(("src", "dst"), None, None, None),
            P(("src", "dst"), None, None),
            P(("src", "dst"), None),
            P(("src", "dst")),
            P("dst", "src"),
            P("src", "dst"),
            P(None, ("src", "dst")),
            P(),
        ),
        out_specs=P("dst", "src"),
        check_vma=False,
    )
```

```python
import functools

import jax
import jax.numpy as jnp
from jax import lax
from jax.experimental import pallas as pl
from jax.experimental.pallas import tpu as pltpu
from jax.sharding import PartitionSpec as P

BI = 128
BJ = 128
BT = 32
MESH = pl.DeviceIdType.MESH


def greet(n_src, n_dst):
    src, dst = lax.axis_index("src"), lax.axis_index("dst")
    barrier = pltpu.get_barrier_semaphore()
    for step in range(1, n_dst):
        peer = (src, lax.rem(dst + step, n_dst))
        pl.semaphore_signal(barrier, inc=1, device_id=peer, device_id_type=MESH)
    for step in range(1, n_src):
        peer = (lax.rem(src + step, n_src), dst)
        pl.semaphore_signal(barrier, inc=1, device_id=peer, device_id_type=MESH)
    pl.semaphore_wait(barrier, n_dst - 1 + n_src - 1)
    return src, dst


def gather_kernel(n_src, n_dst, a_ref, b_ref, c_ref, a_all, b_all, c_all,
                  own_sem, a_send, a_recv, b_send, b_recv, c_send, c_recv, h_send, h_recv):
    src, dst = lax.axis_index("src"), lax.axis_index("dst")
    own = [
        pltpu.make_async_copy(a_ref, a_all.at[dst], own_sem.at[0]),
        pltpu.make_async_copy(b_ref, b_all.at[src], own_sem.at[1]),
        pltpu.make_async_copy(c_ref, c_all.at[src, dst], own_sem.at[2]),
    ]
    for copy in own:
        copy.start()
    greet(n_src, n_dst)

    def remote(source, target, send, recv, peer):
        return pltpu.make_async_remote_copy(
            src_ref=source, dst_ref=target, send_sem=send, recv_sem=recv,
            device_id=peer, device_id_type=MESH)

    hours, early, late, rest = [], [], [], []
    for step in range(1, n_src):
        peer = (lax.rem(src + step, n_src), dst)
        hours.append(remote(c_ref, c_all.at[src, dst], c_send.at[step - 1], c_recv.at[step - 1], peer))
        hours[-1].start()
    src_twin = (src + 1 - 2 * lax.rem(src, 2), dst)
    dst_twin = (src, dst + 1 - 2 * lax.rem(dst, 2))
    for step in range(1, n_src // 2):
        peer = (lax.rem(src + 2 * step, n_src), dst)
        early.append(remote(b_ref, b_all.at[src], b_send.at[step], b_recv.at[step], peer))
        early[-1].start()
    for step in range(1, n_dst // 2):
        peer = (src, lax.rem(dst + 2 * step, n_dst))
        early.append(remote(a_ref, a_all.at[dst], a_send.at[step], a_recv.at[step], peer))
        early[-1].start()
    late.append(remote(b_ref, b_all.at[src], b_send.at[0], b_recv.at[0], src_twin))
    late.append(remote(a_ref, a_all.at[dst], a_send.at[0], a_recv.at[0], dst_twin))
    for copy in late:
        copy.start()
    for copy in own:
        copy.wait()
    for copy in hours:
        copy.wait()
    for step in range(1, n_dst):
        peer = (src, lax.rem(dst + step, n_dst))
        rest.append(remote(c_all.at[:, dst], c_all.at[:, dst], h_send.at[step - 1], h_recv.at[step - 1], peer))
        rest[-1].start()
    for step in range(1, n_dst // 2):
        early[n_src // 2 - 2 + step].wait()
        block = a_all.at[lax.rem(dst + n_dst - 2 * step, n_dst)]
        lane = n_dst // 2 + step - 1
        late.append(remote(block, block, a_send.at[lane], a_recv.at[lane], dst_twin))
        late[-1].start()
    for step in range(1, n_src // 2):
        early[step - 1].wait()
        block = b_all.at[lax.rem(src + n_src - 2 * step, n_src)]
        lane = n_src // 2 + step - 1
        late.append(remote(block, block, b_send.at[lane], b_recv.at[lane], src_twin))
        late[-1].start()
    for copy in late + rest:
        copy.wait()


def gather_all(n_src, n_dst, a, b, c):
    vmem = pl.BlockSpec(memory_space=pltpu.VMEM)
    dma = pltpu.SemaphoreType.DMA
    return pl.pallas_call(
        functools.partial(gather_kernel, n_src, n_dst),
        out_shape=(
            jax.ShapeDtypeStruct((n_dst,) + a.shape, a.dtype),
            jax.ShapeDtypeStruct((n_src,) + b.shape, b.dtype),
            jax.ShapeDtypeStruct((n_src, n_dst) + c.shape, c.dtype),
        ),
        in_specs=[vmem] * 3,
        out_specs=(vmem,) * 3,
        scratch_shapes=[
            dma((3,)), dma((n_dst - 1,)), dma((n_dst - 1,)), dma((n_src - 1,)), dma((n_src - 1,)),
            dma((n_src - 1,)), dma((n_src - 1,)), dma((n_dst - 1,)), dma((n_dst - 1,)),
        ],
        compiler_params=pltpu.CompilerParams(collective_id=0, has_side_effects=True),
        name="gather_factors",
    )(a, b, c)


def split(x):
    high = x.astype(jnp.bfloat16)
    return high, (x - high.astype(jnp.float32)).astype(jnp.bfloat16)


def dot(x, y, contract):
    return lax.dot_general(x, y, (contract, ((), ())), preferred_element_type=jnp.float32)


NN = ((1,), (0,))
NT = ((1,), (1,))
CHUNK = 16


def slot_kernel(n_dst, where_ref, count_ref, values_ref, until_ref, a_ref, b_ref, c_ref, core_ref,
                out_ref, first_ref, a_rows):
    n = pl.program_id(0)
    rank_a = a_rows.shape[0]
    half = rank_a // 2
    each = rank_a // n_dst

    @pl.when(n >= count_ref[0])
    def _():
        out_ref[...] = jnp.zeros_like(out_ref)

    @pl.when(n < count_ref[0])
    def _():
        hour = where_ref[n, 2]
        c_rows = c_ref[pl.ds(pl.multiple_of(hour * BT, BT), BT), :]
        first = dot(c_rows, core_ref[...], NT)
        for pair in range(half):
            first_ref[pl.ds(pair, BT, stride=half), :] = first[:, pair * 128:(pair + 1) * 128]
        b = b_ref[...]
        none = jnp.zeros_like(b)
        b_top = jnp.concatenate([b, none], axis=1)
        b_low = jnp.concatenate([none, b], axis=1)
        b_wide = jnp.concatenate([b_top, b_low, b_top, b_low], axis=0)
        a_rows[...] = a_ref[...].astype(jnp.float32)
        a_even = a_rows[pl.ds(0, half, stride=2), :]
        a_odd = a_rows[pl.ds(1, half, stride=2), :]
        a_cols = jnp.concatenate([a_even, a_odd, a_even, a_odd], axis=0).T.astype(jnp.bfloat16)
        lane = lax.broadcasted_iota(jnp.int32, (half, 128), 1)
        left = lane < 64
        until = until_ref[0]

        def step(chunk, total):
            start = chunk * CHUNK
            f = first_ref[pl.ds(pl.multiple_of(start * half, half), CHUNK * half), :]
            f_high, f_low = split(f)
            second = dot(jnp.concatenate([f_high, f_low], axis=1), b_wide, NN)
            s_high, s_low = split(second)
            for two in range(0, CHUNK, 2):
                def column(t):
                    rows = slice(t * half, (t + 1) * half)
                    return jnp.concatenate(
                        [s_high[rows, :128], s_high[rows, 128:], s_low[rows, :128], s_low[rows, 128:]], axis=0)
                rebuilt = dot(a_cols, jnp.concatenate([column(two), column(two + 1)], axis=1), NN)
                parts = []
                for side in range(2):
                    seen = values_ref[0, start + two + side].astype(jnp.float32)
                    guess = rebuilt[:, side * 128:(side + 1) * 128]
                    parts.append(jnp.where(start + two + side < until, seen, guess).astype(jnp.bfloat16))
                along = dot(b, jnp.concatenate(parts, axis=0), NT)
                along_high, along_low = split(along)
                core_high, core_low, turn_high, turn_low = [], [], [], []
                for side in range(2):
                    rows = slice((two + side) * half, (two + side + 1) * half)
                    cols = slice(side * 128, (side + 1) * 128)
                    fh, fl = f_high[rows], f_low[rows]
                    nil = jnp.zeros_like(fh)
                    core_high.append(jnp.concatenate([jnp.where(left, fh, nil), jnp.where(left, nil, fh)], axis=0))
                    core_low.append(jnp.concatenate([jnp.where(left, fl, nil), jnp.where(left, nil, fl)], axis=0))
                    turn_high += [along_high[:, cols]] * 2
                    turn_low += [along_low[:, cols]] * 2
                turn_high = jnp.concatenate(turn_high, axis=0)
                turn_low = jnp.concatenate(turn_low, axis=0)
                core_high = jnp.concatenate(core_high, axis=1)
                core_low = jnp.concatenate(core_low, axis=1)
                both = dot(jnp.concatenate([core_high, core_low], axis=0), turn_high, NN)
                total = total + both[:rank_a] + both[rank_a:] + dot(core_high, turn_low, NN)
            return total

        total = lax.fori_loop(0, BT // CHUNK, step, jnp.zeros((rank_a, BI), jnp.float32))
        a_rows[pl.ds(0, half, stride=2), :] = total[:half]
        a_rows[pl.ds(1, half, stride=2), :] = total[half:]
        for q in range(n_dst):
            out_ref[q, 0] = a_rows[q * each:(q + 1) * each, :]


def slot_shares(n_dst, where, count, values, until, a, b, c, core):
    slots = values.shape[0]
    rank_a = a.shape[0]

    def alive(n, count_ref):
        return jnp.minimum(n, count_ref[0] - 1)

    return pl.pallas_call(
        functools.partial(slot_kernel, n_dst),
        out_shape=jax.ShapeDtypeStruct((n_dst, slots, rank_a // n_dst, BI), jnp.float32),
        grid_spec=pltpu.PrefetchScalarGridSpec(
            num_scalar_prefetch=2,
            grid=(slots,),
            in_specs=[
                pl.BlockSpec((1, BT, BI, BJ), lambda n, w, c: (alive(n, c), 0, 0, 0)),
                pl.BlockSpec((1, BI, BJ), lambda n, w, c: (alive(n, c), 0, 0)),
                pl.BlockSpec((rank_a, BI), lambda n, w, c: (0, w[alive(n, c), 0])),
                pl.BlockSpec((b.shape[0], BJ), lambda n, w, c: (0, w[alive(n, c), 1])),
                pl.BlockSpec(c.shape, lambda n, w, c: (0, 0)),
                pl.BlockSpec(core.shape, lambda n, w, c: (0, 0)),
            ],
            out_specs=pl.BlockSpec((n_dst, 1, rank_a // n_dst, BI), lambda n, w, c: (0, n, 0, 0)),
            scratch_shapes=[
                pltpu.VMEM((BT * rank_a // 2, 128), jnp.float32),
                pltpu.VMEM((rank_a, BI), jnp.float32),
            ],
        ),
        name="slot_shares",
    )(where, count, values, until, a, b, c, core)


def sum_kernel(n_dst, share_ref, ids_ref, out_ref, shares, ids, own_sem, s_send, s_recv, i_send, i_recv):
    src, dst = lax.axis_index("src"), lax.axis_index("dst")
    own = [
        pltpu.make_async_copy(share_ref.at[dst], shares.at[dst], own_sem.at[0]),
        pltpu.make_async_copy(ids_ref, ids.at[dst], own_sem.at[1]),
    ]
    for copy in own:
        copy.start()
    greet(1, n_dst)
    copies = []
    for step in range(1, n_dst):
        to = lax.rem(dst + step, n_dst)
        for source, target, send, recv in (
            (share_ref.at[to], shares.at[dst], s_send, s_recv),
            (ids_ref, ids.at[dst], i_send, i_recv),
        ):
            copies.append(pltpu.make_async_remote_copy(
                src_ref=source, dst_ref=target, send_sem=send.at[step - 1], recv_sem=recv.at[step - 1],
                device_id=(src, to), device_id_type=MESH))
            copies[-1].start()
    for copy in own + copies:
        copy.wait()
    slots, each = shares.shape[1], shares.shape[2]

    def block(s, carry):
        def device(q, total):
            for n in range(slots):
                mine = jnp.broadcast_to(ids[q, n:n + 1, :], (each, BI)) == s
                total = total + jnp.where(mine, shares[q, n], 0.0)
            return total
        total = jnp.zeros((each, BI), jnp.float32)
        total = lax.fori_loop(0, n_dst, device, total)
        out_ref[:, pl.ds(pl.multiple_of(s * BI, BI), BI)] = total
        return carry

    lax.fori_loop(0, out_ref.shape[1] // BI, block, 0)


def sum_shares(n_dst, shares, ids, columns):
    vmem = pl.BlockSpec(memory_space=pltpu.VMEM)
    dma = pltpu.SemaphoreType.DMA
    return pl.pallas_call(
        functools.partial(sum_kernel, n_dst),
        out_shape=jax.ShapeDtypeStruct((shares.shape[2], columns), jnp.float32),
        in_specs=[vmem] * 2,
        out_specs=vmem,
        scratch_shapes=[
            pltpu.VMEM(shares.shape, jnp.float32),
            pltpu.VMEM((n_dst,) + ids.shape, jnp.int32),
            dma((2,)), dma((n_dst - 1,)), dma((n_dst - 1,)), dma((n_dst - 1,)), dma((n_dst - 1,)),
        ],
        compiler_params=pltpu.CompilerParams(collective_id=1, has_side_effects=True),
        name="sum_shares",
    )(shares, ids)


def on_device(n_src, n_dst, values, until, blocks, count, a_factor, b_factor, c_factor, core):
    rank_a, rank_b, rank_c = core.shape
    slots = values.shape[0]
    src_blocks = a_factor.shape[1] // BI
    dst_blocks = b_factor.shape[1] // BJ
    base = jnp.stack([
        lax.axis_index("src") * src_blocks, lax.axis_index("dst") * dst_blocks, jnp.zeros((), jnp.int32)])
    where = blocks - base.astype(jnp.int32)[None, :]
    flat = core.reshape(rank_a * rank_b, rank_c)
    high = lax.reduce_precision(flat, 8, 7)
    rest = flat - high
    mid = lax.reduce_precision(rest, 8, 7)
    core_parts = jnp.concatenate([high, mid, rest - mid], axis=1).astype(jnp.bfloat16)
    a_all, b_all, c_all = gather_all(n_src, n_dst, a_factor, b_factor, c_factor.T.astype(jnp.float32))
    a_all = a_all.reshape(rank_a, -1)
    b_all = b_all.reshape(rank_b, -1)
    c_all = c_all.reshape(-1, rank_c).astype(jnp.bfloat16)
    c_all = jnp.concatenate([c_all] * 3, axis=1)
    shares = slot_shares(n_dst, where, count, values, until, a_all, b_all, c_all, core_parts)
    live = jnp.arange(slots, dtype=jnp.int32) < count[0]
    ids = jnp.broadcast_to(jnp.where(live, where[:, 0], -1)[:, None], (slots, BI))
    return sum_shares(n_dst, shares, ids, a_factor.shape[1])


def solution(mesh):
    return jax.shard_map(
        functools.partial(on_device, mesh.shape["src"], mesh.shape["dst"]),
        mesh=mesh,
        in_specs=(
            P(("src", "dst"), None, None, None),
            P(("src", "dst"), None, None),
            P(("src", "dst"), None),
            P(("src", "dst")),
            P("dst", "src"),
            P("src", "dst"),
            P(None, ("src", "dst")),
            P(),
        ),
        out_specs=P("dst", "src"),
        check_vma=False,
    )
```
